32 devices in a mesh: group: 4 (over y, core), region: 8 (over z, x).
Axes of the slice: x: 2, y: 2, z: 4, core: 2. Of those that a mesh axis runs over, the one named last changes fastest.
Arguments:
- observed: float32 [65536], P(('group', 'region')), may hold values from -6 to 6
- noise_precision: float32 [65536], P(('group', 'region')), may hold values from 0.25 to 4
- mid_basis: float32 [65536, 512], P(('group', 'region')), may hold values from -0.077339804 to 0.077339804
- root_basis: float32 [65536, 512], P(('group', 'region')), may hold values from -0.038669902 to 0.038669902
- mid_prior: float32 [4, 512], P('group'), may hold values from 0.3 to 3
- root_prior: float32 [512], replicated, may hold values from 0.3 to 3
- leaf_count: int32 [4, 8], P('group', 'region'), may hold values from 1024 to 2048, as said below
Outputs:
- root_weight_means: float32 [512], replicated
- middle_weight_means: float32 [4, 512], P('group', 'region')
- leaf_fit: float32 [65536], P(('group', 'region'))
The draws below stay inside these ranges and needn't reach their ends.
Inputs may be any that keep to these rules, and one draw needn't show every extreme that they name: `leaf_count`: every entry lies between 1024 and 2048, and some region has all 2048 slots live.
All inputs are finite; a program needn't handle non-finite values.
Results may differ from the reference program's by a relative error of at most 0.0012.
Values sent between devices are 32-bit elements; how exact they have to be, the bound alone decides.
A program may use at most 64 MiB of HBM per device.

```python
import math
import jax
import jax.numpy as jnp
from jax import lax

L = 2048
M = 512
R = 512
GROUPS = 4
REGIONS = 8
GROUP_OBS = 16384
OBS = 65536
N_GROUP = 4
N_REGION = 8


energy_level = 8.0


clip_level = 3.5


shared_part = 0.8


fresh_part = 0.6


mid_stretch_divisor = 1.5


root_stretch_divisor = 6.0


def draw_leaf_count(key, part):
    counts = jax.random.randint(key, (GROUPS * REGIONS,), L // 2, L + 1)
    chosen = jax.random.randint(jax.random.fold_in(key, 7), (), 0, GROUPS * REGIONS)
    counts = jnp.where(jnp.arange(GROUPS * REGIONS) == chosen, L, counts)
    return counts.reshape(GROUPS, REGIONS).astype(jnp.int32)


def knot_mixing(base_key, knot_count, divisor):
    points = jax.random.uniform(base_key, (knot_count, 2), jnp.float32)
    offsets = points[:, None, :] - points[None, :, :]
    distance = jnp.sqrt(jnp.sum(offsets * offsets, axis=-1))
    stretch = math.sqrt(knot_count) / divisor
    scaled = distance * stretch
    kernel = (1.0 + scaled) * jnp.exp(-scaled)
    return kernel / jnp.sqrt(jnp.sum(kernel * kernel, axis=0, keepdims=True))


def latent_block(row_key, width):
    return jax.random.normal(row_key, (GROUP_OBS, width), jnp.float32)


def shared_latent(key, group_index):
    return latent_block(jax.random.fold_in(jax.random.fold_in(key, 41), group_index), max(M, R))


def basis_rows(latent, mixing, spread):
    rows = jnp.dot(latent, mixing, precision=lax.Precision.HIGHEST, preferred_element_type=jnp.float32) * spread
    limit = clip_level * spread
    return jnp.clip(rows, -limit, limit)


def draw_mid_basis(key, part):
    base_key = jax.random.fold_in(key, 11)
    spread = math.sqrt(energy_level / GROUP_OBS)

    def one_group(group_index):
        mixing = knot_mixing(jax.random.fold_in(base_key, 2 * group_index + 1), M, mid_stretch_divisor)
        latent = shared_latent(key, group_index)[:, :M]
        return basis_rows(latent, mixing, spread)
    return lax.map(one_group, jnp.arange(GROUPS, dtype=jnp.int32)).reshape(OBS, M)


def draw_root_basis(key, part):
    base_key = jax.random.fold_in(key, 23)
    mixing = knot_mixing(jax.random.fold_in(key, 29), R, root_stretch_divisor)
    spread = math.sqrt(energy_level / OBS)

    def one_group(group_index):
        fresh = latent_block(jax.random.fold_in(base_key, group_index), R)
        latent = shared_part * shared_latent(key, group_index)[:, :R] + fresh_part * fresh
        return basis_rows(latent, mixing, spread)
    return lax.map(one_group, jnp.arange(GROUPS, dtype=jnp.int32)).reshape(OBS, R)


def levels(stream_key, dims, pieces, smallest, top_value):
    gain, own = 1.0, jax.random.fold_in(stream_key, 6)
    for position, blocks in pieces:
        draws = jnp.exp(jax.random.uniform(jax.random.fold_in(own, position), (blocks,), jnp.float32, smallest / len(pieces), top_value / len(pieces)))
        gain = gain * jnp.repeat(draws, dims[position] // blocks).reshape([-1 if axis == position else 1 for axis in range(len(dims))])
    return gain


def centred(key, dims, scale, most, shards=(), held_as=jnp.bfloat16):
    entries = scale * jax.random.normal(key, dims, jnp.float32)
    if shards:
        entries = entries * levels(key, dims, shards, -0.22, 0.18)
    return jnp.clip(entries, -most, most).astype(held_as)


def setup_inputs(seed: int = 0) -> dict:
    splits = jax.random.split(jax.random.key(seed), 8)
    return {
        "observed": centred(splits[0], (OBS,), 1.0, 6.0, ((0, 32),), jnp.float32),
        "noise_precision": jnp.clip(jnp.exp(math.log(4.0) - 2.7725887 * jax.random.uniform(splits[1], (OBS,), jnp.float32) ** levels(splits[1], (OBS,), ((0, 32),), -0.2, 0.2)), 0.25, 4.0),
        "mid_basis": draw_mid_basis(jax.random.fold_in(splits[7], 71), 0),
        "root_basis": draw_root_basis(jax.random.fold_in(splits[7], 71), 0),
        "mid_prior": jnp.clip(jnp.exp(math.log(3.0) - 2.3025851 * jax.random.uniform(splits[4], (GROUPS, M), jnp.float32) ** levels(splits[4], (GROUPS, M), ((0, 4),), -0.2, 0.2)), 0.3, 3.0),
        "root_prior": jnp.clip(jnp.exp(jax.random.uniform(splits[5], (R,), jnp.float32, math.log(0.3), math.log(3.0))), 0.3, 3.0),
        "leaf_count": draw_leaf_count(jax.random.fold_in(splits[7], 71), 0),
    }


highest_precision = lax.Precision.HIGHEST

def inner_gram(former, latter):
    return lax.dot_general(former.astype(jnp.float32), latter.astype(jnp.float32), (((0,), (0,)), ((), ())), precision=highest_precision, preferred_element_type=jnp.float32)

def cholesky_solve(factor, rhs):
    column = rhs.ndim == 1
    matrix = rhs[:, None] if column else rhs
    lower_solved = lax.linalg.triangular_solve(factor, matrix, left_side=True, lower=True)
    result = lax.linalg.triangular_solve(factor, lower_solved, left_side=True, lower=True, transpose_a=True)
    return result[:, 0] if column else result

def reference(observed, noise_precision, mid_basis, root_basis, mid_prior, root_prior, leaf_count):
    per_group = L * N_REGION
    live = (jnp.arange(L, dtype=jnp.int32)[None, None, :] < leaf_count[:, :, None]).astype(jnp.float32)
    weight = noise_precision.reshape(N_GROUP, per_group) * live.reshape(N_GROUP, per_group)
    values = observed.reshape(N_GROUP, per_group)
    mid_rows = mid_basis.reshape(N_GROUP, per_group, M)
    root_rows = root_basis.reshape(N_GROUP, per_group, R)

    def group_contributions(items):
        values_g, weight_g, mid_g, root_g, prior_g = items
        weighted_obs = values_g * weight_g
        weighted_mid = mid_g * weight_g[:, None]
        mid_gram = inner_gram(weighted_mid, mid_g) + jnp.diag(prior_g)
        cross = inner_gram(weighted_mid, root_g)
        mid_rhs = jnp.dot(weighted_obs.astype(jnp.float32), mid_g.astype(jnp.float32), precision=highest_precision, preferred_element_type=jnp.float32)
        root_gram = inner_gram(root_g * weight_g[:, None], root_g)
        root_rhs = jnp.dot(weighted_obs.astype(jnp.float32), root_g.astype(jnp.float32), precision=highest_precision, preferred_element_type=jnp.float32)
        factor = jnp.linalg.cholesky(mid_gram)
        solved_cross_terms = cholesky_solve(factor, cross)
        solved_right_hand = cholesky_solve(factor, mid_rhs)
        reduced_gram = root_gram - inner_gram(cross, solved_cross_terms)
        reduced_rhs = root_rhs - jnp.dot(solved_right_hand.astype(jnp.float32), cross.astype(jnp.float32), precision=highest_precision, preferred_element_type=jnp.float32)
        return (reduced_gram, reduced_rhs, solved_cross_terms, solved_right_hand)
    reduced_gram, reduced_rhs, solved_cross_terms, solved_right_hand = lax.map(group_contributions, (values, weight, mid_rows, root_rows, mid_prior))
    root_matrix = jnp.sum(reduced_gram, axis=0) + jnp.diag(root_prior)
    root_vector = jnp.sum(reduced_rhs, axis=0)
    root_factor = jnp.linalg.cholesky(root_matrix)
    root_weight_means = cholesky_solve(root_factor, root_vector)
    middle_weight_means = solved_right_hand - jnp.einsum('wok,k->wo', solved_cross_terms, root_weight_means, precision=highest_precision)
    fit_mid = jnp.einsum('gnm,gm->gn', mid_rows, middle_weight_means, precision=highest_precision).reshape(-1)
    fit_root = jnp.dot(root_basis.astype(jnp.float32), root_weight_means.astype(jnp.float32), precision=highest_precision, preferred_element_type=jnp.float32)
    return (root_weight_means, middle_weight_means, fit_mid + fit_root)
```

```python
import functools

import jax
import jax.numpy as jnp
from jax import lax
from jax.experimental import pallas as pl
from jax.experimental.pallas import tpu as pltpu
from jax.sharding import PartitionSpec as P

HIGHEST = lax.Precision.HIGHEST
HIGH = lax.Precision.HIGH
BLOCK = 128
PANEL = 8


def inner_gram(former, latter, precision):
    return lax.dot_general(
        former,
        latter,
        (((0,), (0,)), ((), ())),
        precision=precision,
        preferred_element_type=jnp.float32,
    )


def vector_product(vector, matrix):
    return jnp.dot(vector, matrix, precision=HIGHEST, preferred_element_type=jnp.float32)


def mxu(a, b):
    return jnp.dot(a, b, precision=HIGHEST, preferred_element_type=jnp.float32)


def negated_inverse(groups):
    count = len(groups)
    shape = (PANEL, count * PANEL)
    lane = lax.broadcasted_iota(jnp.int32, shape, 1)
    sub = lax.broadcasted_iota(jnp.int32, shape, 0)
    for p in range(count):
        rows = groups[p]
        first = p * PANEL
        inside = (lane >= first) & (lane < first + PANEL)
        cols = [jnp.broadcast_to(rows[:, first + k : first + k + 1], shape) for k in range(PANEL)]
        work = jnp.where(lane == first + sub, -1.0, jnp.where(inside, 0.0, rows))
        for k in range(PANEL):
            inv = 1.0 / jnp.broadcast_to(cols[k][k : k + 1, :], shape)
            own = sub == k
            factor = cols[k]
            for j in range(k + 1, PANEL):
                pivot_row = jnp.broadcast_to(cols[j][k : k + 1, :], shape) * inv
                cols[j] = jnp.where(own, pivot_row, cols[j] - factor * pivot_row)
            pivot_row = jnp.broadcast_to(work[k : k + 1, :], shape) * inv
            work = jnp.where(own, pivot_row, work - factor * pivot_row)
        spread = [jnp.broadcast_to(work[k : k + 1, :], shape) for k in range(PANEL)]
        order = [(p + 1 + i) % count for i in range(count - 1)]
        for i in order:
            value = jnp.where(inside, 0.0, groups[i])
            for k in range(PANEL):
                column = jnp.broadcast_to(groups[i][:, first + k : first + k + 1], shape)
                value = value - column * spread[k]
            groups[i] = value
        groups[p] = work
    return groups


def eliminate(a_ref, b_ref, inv_ref):
    size = a_ref.shape[0]
    blocks = size // BLOCK

    def step(kb, carry):
        start = pl.multiple_of(kb * BLOCK, BLOCK)
        own = pl.ds(start, BLOCK)
        diagonal = a_ref[own, own]
        groups = [diagonal[i * PANEL : (i + 1) * PANEL, :] for i in range(BLOCK // PANEL)]
        groups = negated_inverse(groups)
        for i, value in enumerate(groups):
            inv_ref[i * PANEL : (i + 1) * PANEL, :] = -value
        inverse = inv_ref[...]
        row_a = mxu(inverse, a_ref[own, :])
        row_b = mxu(inverse, b_ref[own, :])
        for i in range(blocks):
            @pl.when(i != kb)
            def _():
                at = pl.ds(i * BLOCK, BLOCK)
                left = a_ref[at, own]
                a_ref[at, :] = a_ref[at, :] - mxu(left, row_a)
                b_ref[at, :] = b_ref[at, :] - mxu(left, row_b)
        a_ref[own, :] = row_a
        b_ref[own, :] = row_b
        return carry

    lax.fori_loop(0, blocks, step, 0)


def add_diagonal(a_ref, prior_ref):
    size = a_ref.shape[0]
    rows = lax.broadcasted_iota(jnp.int32, (size, size), 0)
    cols = lax.broadcasted_iota(jnp.int32, (size, size), 1)
    return a_ref[...] + jnp.where(rows == cols, prior_ref[...], 0.0)


def mid_kernel(gram_ref, prior_ref, rhs_ref, solved_ref, schur_ref, a_ref, inv_ref):
    knots = gram_ref.shape[0]
    root = schur_ref.shape[0]
    a_ref[...] = add_diagonal(gram_ref, prior_ref)
    solved_ref[...] = rhs_ref[...]
    eliminate(a_ref, solved_ref, inv_ref)
    schur_ref[...] = lax.dot_general(
        rhs_ref[:, :root],
        solved_ref[...],
        (((0,), (0,)), ((), ())),
        precision=HIGHEST,
        preferred_element_type=jnp.float32,
    )


def root_kernel(gram_ref, prior_ref, rhs_ref, solved_ref, a_ref, inv_ref):
    a_ref[...] = add_diagonal(gram_ref, prior_ref)
    solved_ref[...] = rhs_ref[...]
    eliminate(a_ref, solved_ref, inv_ref)


def mid_solve(gram, prior, rhs, root):
    knots, width = rhs.shape
    return pl.pallas_call(
        mid_kernel,
        out_shape=(
            jax.ShapeDtypeStruct((knots, width), jnp.float32),
            jax.ShapeDtypeStruct((root, width), jnp.float32),
        ),
        scratch_shapes=[
            pltpu.VMEM((knots, knots), jnp.float32),
            pltpu.VMEM((BLOCK, BLOCK), jnp.float32),
        ],
        cost_estimate=pl.CostEstimate(flops=10**10, bytes_accessed=10**7, transcendentals=0),
        name="mid_solve",
    )(gram, prior[None, :], rhs)


def root_solve(gram, prior, rhs):
    knots, width = rhs.shape
    return pl.pallas_call(
        root_kernel,
        out_shape=jax.ShapeDtypeStruct((knots, width), jnp.float32),
        scratch_shapes=[
            pltpu.VMEM((knots, knots), jnp.float32),
            pltpu.VMEM((BLOCK, BLOCK), jnp.float32),
        ],
        name="root_solve",
    )(gram, prior[None, :], rhs)


def pad_columns(vector):
    return jnp.pad(vector[:, None], ((0, 0), (0, BLOCK - 1)))


def on_device(observed, noise_precision, mid_basis, root_basis, mid_prior, root_prior, leaf_count):
    leaf_slots = observed.shape[0]
    knots_mid = mid_basis.shape[1]
    root_knots = root_basis.shape[1]
    live = (jnp.arange(leaf_slots, dtype=jnp.int32) < leaf_count[0, 0]).astype(jnp.float32)
    weight = noise_precision * live
    weighted_obs = observed * weight
    weighted_mid = mid_basis * weight[:, None]
    mid_gram = inner_gram(weighted_mid, mid_basis, HIGH)
    cross_gram = inner_gram(weighted_mid, root_basis, HIGH)
    mid_rhs = vector_product(weighted_obs, mid_basis)
    root_gram = inner_gram(root_basis * weight[:, None], root_basis, HIGH)
    root_rhs = vector_product(weighted_obs, root_basis)
    region = lax.axis_index("region")
    regions = lax.axis_size("region")
    group_gram, group_cross, group_rhs = lax.psum((mid_gram, cross_gram, mid_rhs), "region")
    total_root, total_root_rhs = lax.psum((root_gram, root_rhs), ("group", "region"))
    right = jnp.concatenate([group_cross, pad_columns(group_rhs)], axis=1)
    solved, schur = mid_solve(group_gram, mid_prior[0], right, root_knots)
    total_schur = lax.psum(schur, "group")
    root_matrix = total_root - total_schur[:, :root_knots]
    root_vector = total_root_rhs - total_schur[:, root_knots]
    root_weight_means = root_solve(root_matrix, root_prior, pad_columns(root_vector))[:, 0]
    group_mid = solved[:, root_knots] - jnp.dot(
        solved[:, :root_knots],
        root_weight_means,
        precision=HIGHEST,
        preferred_element_type=jnp.float32,
    )
    mid_slab = knots_mid // regions
    middle_weight_means = lax.dynamic_slice_in_dim(group_mid, region * mid_slab, mid_slab, 0)[
        None, :
    ]
    fit_mid = jnp.dot(mid_basis, group_mid, precision=HIGHEST, preferred_element_type=jnp.float32)
    fit_root = jnp.dot(
        root_basis, root_weight_means, precision=HIGHEST, preferred_element_type=jnp.float32
    )
    return (root_weight_means, middle_weight_means, fit_mid + fit_root)


def solution(mesh):
    return jax.shard_map(
        on_device,
        mesh=mesh,
        in_specs=(
            P(("group", "region")),
            P(("group", "region")),
            P(("group", "region"), None),
            P(("group", "region"), None),
            P("group", None),
            P(),
            P("group", "region"),
        ),
        out_specs=(P(), P("group", "region"), P(("group", "region"))),
        check_vma=False,
    )
```

```python
import functools

import jax
import jax.numpy as jnp
from jax import lax
from jax.experimental import pallas as pl
from jax.experimental.pallas import tpu as pltpu
from jax.sharding import PartitionSpec as P

HIGHEST = lax.Precision.HIGHEST
HIGH = lax.Precision.HIGH
BLOCK = 128
PANEL = 8


def inner_gram(former, latter, precision):
    return lax.dot_general(
        former,
        latter,
        (((0,), (0,)), ((), ())),
        precision=precision,
        preferred_element_type=jnp.float32,
    )


def vector_product(vector, matrix):
    return jnp.dot(vector, matrix, precision=HIGHEST, preferred_element_type=jnp.float32)


def mxu(a, b):
    return jnp.dot(a, b, precision=HIGHEST, preferred_element_type=jnp.float32)


def negated_inverse(groups):
    count = len(groups)
    shape = (PANEL, count * PANEL)
    lane = lax.broadcasted_iota(jnp.int32, shape, 1)
    sub = lax.broadcasted_iota(jnp.int32, shape, 0)
    for p in range(count):
        rows = groups[p]
        first = p * PANEL
        inside = (lane >= first) & (lane < first + PANEL)
        cols = [jnp.broadcast_to(rows[:, first + k : first + k + 1], shape) for k in range(PANEL)]
        work = jnp.where(lane == first + sub, -1.0, jnp.where(inside, 0.0, rows))
        for k in range(PANEL):
            inv = 1.0 / jnp.broadcast_to(cols[k][k : k + 1, :], shape)
            own = sub == k
            factor = cols[k]
            for j in range(k + 1, PANEL):
                pivot_row = jnp.broadcast_to(cols[j][k : k + 1, :], shape) * inv
                cols[j] = jnp.where(own, pivot_row, cols[j] - factor * pivot_row)
            pivot_row = jnp.broadcast_to(work[k : k + 1, :], shape) * inv
            work = jnp.where(own, pivot_row, work - factor * pivot_row)
        spread = [jnp.broadcast_to(work[k : k + 1, :], shape) for k in range(PANEL)]
        order = [(p + 1 + i) % count for i in range(count - 1)]
        for i in order:
            value = jnp.where(inside, 0.0, groups[i])
            for k in range(PANEL):
                column = jnp.broadcast_to(groups[i][:, first + k : first + k + 1], shape)
                value = value - column * spread[k]
            groups[i] = value
        groups[p] = work
    return groups


def eliminate(a_ref, b_ref, inv_ref):
    size = a_ref.shape[0]
    blocks = size // BLOCK

    def step(kb, carry):
        start = pl.multiple_of(kb * BLOCK, BLOCK)
        own = pl.ds(start, BLOCK)
        diagonal = a_ref[own, own]
        groups = [diagonal[i * PANEL : (i + 1) * PANEL, :] for i in range(BLOCK // PANEL)]
        groups = negated_inverse(groups)
        for i, value in enumerate(groups):
            inv_ref[i * PANEL : (i + 1) * PANEL, :] = -value
        inverse = inv_ref[...]
        row_a = mxu(inverse, a_ref[own, :])
        row_b = mxu(inverse, b_ref[own, :])
        for i in range(blocks):
            @pl.when(i != kb)
            def _():
                at = pl.ds(i * BLOCK, BLOCK)
                left = a_ref[at, own]
                a_ref[at, :] = a_ref[at, :] - mxu(left, row_a)
                b_ref[at, :] = b_ref[at, :] - mxu(left, row_b)
        a_ref[own, :] = row_a
        b_ref[own, :] = row_b
        return carry

    lax.fori_loop(0, blocks, step, 0)


def add_diagonal(a_ref, prior_ref):
    size = a_ref.shape[0]
    rows = lax.broadcasted_iota(jnp.int32, (size, size), 0)
    cols = lax.broadcasted_iota(jnp.int32, (size, size), 1)
    return a_ref[...] + jnp.where(rows == cols, prior_ref[...], 0.0)


def invert(a_ref, inv_ref):
    size = a_ref.shape[0]
    blocks = size // BLOCK
    rows = lax.broadcasted_iota(jnp.int32, (BLOCK, BLOCK), 0)
    cols = lax.broadcasted_iota(jnp.int32, (BLOCK, BLOCK), 1)
    unit = jnp.where(rows == cols, 1.0, 0.0)

    def step(kb, carry):
        start = pl.multiple_of(kb * BLOCK, BLOCK)
        own = pl.ds(start, BLOCK)
        diagonal = a_ref[own, own]
        groups = [diagonal[i * PANEL : (i + 1) * PANEL, :] for i in range(BLOCK // PANEL)]
        groups = negated_inverse(groups)
        for i, value in enumerate(groups):
            inv_ref[i * PANEL : (i + 1) * PANEL, :] = -value
        a_ref[own, own] = unit
        row = mxu(inv_ref[...], a_ref[own, :])
        for i in range(blocks):
            @pl.when(i != kb)
            def _():
                at = pl.ds(i * BLOCK, BLOCK)
                left = a_ref[at, own]
                a_ref[at, own] = jnp.zeros((BLOCK, BLOCK), jnp.float32)
                a_ref[at, :] = a_ref[at, :] - mxu(left, row)
        a_ref[own, :] = row
        return carry

    lax.fori_loop(0, blocks, step, 0)


def mid_kernel(gram_ref, prior_ref, inverse_ref, inv_ref):
    inverse_ref[...] = add_diagonal(gram_ref, prior_ref)
    invert(inverse_ref, inv_ref)


def schur_kernel(
    axis, members, inverse_ref, rhs_ref, slab_ref, root_ref, solved_ref, total_ref,
    work_ref, land_ref, send_sem, recv_sem,
):
    me = lax.axis_index(axis)
    steps = members.bit_length() - 1
    partners = []
    for s in range(steps):
        bit = 1 << s
        partners.append(me + bit * (1 - 2 * ((me // bit) % 2)))
    barrier = pltpu.get_barrier_semaphore()
    for partner in partners:
        pl.semaphore_signal(
            barrier, inc=1, device_id={axis: partner}, device_id_type=pl.DeviceIdType.MESH
        )
    solved_ref[...] = mxu(inverse_ref[...], rhs_ref[...])
    work_ref[0] = root_ref[...] - lax.dot_general(
        slab_ref[...],
        solved_ref[...],
        (((0,), (0,)), ((), ())),
        precision=HIGHEST,
        preferred_element_type=jnp.float32,
    )
    pl.semaphore_wait(barrier, steps)
    for s, partner in enumerate(partners):
        copy = pltpu.make_async_remote_copy(
            src_ref=work_ref.at[s],
            dst_ref=land_ref.at[s],
            send_sem=send_sem.at[s],
            recv_sem=recv_sem.at[s],
            device_id={axis: partner},
            device_id_type=pl.DeviceIdType.MESH,
        )
        copy.start()
        copy.wait()
        if s + 1 < steps:
            work_ref[s + 1] = work_ref[s] + land_ref[s]
        else:
            total_ref[...] = work_ref[s] + land_ref[s]


def root_kernel(gram_ref, prior_ref, rhs_ref, solved_ref, a_ref, inv_ref):
    a_ref[...] = add_diagonal(gram_ref, prior_ref)
    solved_ref[...] = rhs_ref[...]
    eliminate(a_ref, solved_ref, inv_ref)


def mid_inverse(gram, prior):
    knots = gram.shape[0]
    return pl.pallas_call(
        mid_kernel,
        out_shape=jax.ShapeDtypeStruct((knots, knots), jnp.float32),
        scratch_shapes=[pltpu.VMEM((BLOCK, BLOCK), jnp.float32)],
        cost_estimate=pl.CostEstimate(flops=2 * 10**10, bytes_accessed=10**7, transcendentals=0),
        name="mid_inverse",
    )(gram, prior[None, :])


def schur_sum(axis, inverse, rhs, slab, root):
    knots, width = rhs.shape
    members = lax.axis_size(axis)
    steps = members.bit_length() - 1
    return pl.pallas_call(
        functools.partial(schur_kernel, axis, members),
        out_shape=(
            jax.ShapeDtypeStruct((knots, width), jnp.float32),
            jax.ShapeDtypeStruct(root.shape, jnp.float32),
        ),
        scratch_shapes=[
            pltpu.VMEM((steps, *root.shape), jnp.float32),
            pltpu.VMEM((steps, *root.shape), jnp.float32),
            pltpu.SemaphoreType.DMA((steps,)),
            pltpu.SemaphoreType.DMA((steps,)),
        ],
        compiler_params=pltpu.CompilerParams(collective_id=0, has_side_effects=True),
        name="schur_sum",
    )(inverse, rhs, slab, root)


def root_solve(gram, prior, rhs):
    knots, width = rhs.shape
    return pl.pallas_call(
        root_kernel,
        out_shape=jax.ShapeDtypeStruct((knots, width), jnp.float32),
        scratch_shapes=[
            pltpu.VMEM((knots, knots), jnp.float32),
            pltpu.VMEM((BLOCK, BLOCK), jnp.float32),
        ],
        name="root_solve",
    )(gram, prior[None, :], rhs)


def pad_columns(vector):
    return jnp.pad(vector[:, None], ((0, 0), (0, BLOCK - 1)))


def on_device(observed, noise_precision, mid_basis, root_basis, mid_prior, root_prior, leaf_count):
    leaf_slots = observed.shape[0]
    knots_mid = mid_basis.shape[1]
    root_knots = root_basis.shape[1]
    live = (jnp.arange(leaf_slots, dtype=jnp.int32) < leaf_count[0, 0]).astype(jnp.float32)
    weight = noise_precision * live
    weighted_obs = observed * weight
    weighted_mid = mid_basis * weight[:, None]
    mid_gram = inner_gram(weighted_mid, mid_basis, HIGH)
    cross_gram = inner_gram(weighted_mid, root_basis, HIGH)
    mid_rhs = vector_product(weighted_obs, mid_basis)
    root_gram = inner_gram(root_basis * weight[:, None], root_basis, HIGH)
    root_rhs = vector_product(weighted_obs, root_basis)
    region = lax.axis_index("region")
    regions = lax.axis_size("region")
    root_slab = root_knots // regions
    group_gram = lax.psum(mid_gram, "region")
    right, group_gram = lax.optimization_barrier(
        (jnp.concatenate([cross_gram, pad_columns(mid_rhs)], axis=1), group_gram)
    )
    group_right = lax.psum(right, "region")
    own_root = lax.psum_scatter(
        jnp.concatenate([root_gram, pad_columns(root_rhs)], axis=1),
        "region",
        scatter_dimension=0,
        tiled=True,
    )
    inverse = mid_inverse(group_gram, mid_prior[0])
    cross_slab = lax.dynamic_slice_in_dim(group_right, region * root_slab, root_slab, 1)
    solved, own_total = schur_sum("group", inverse, group_right, cross_slab, own_root)
    total = lax.all_gather(own_total, "region", axis=0, tiled=True)
    root_weight_means = root_solve(
        total[:, :root_knots], root_prior, total[:, root_knots:]
    )[:, 0]
    group_mid = solved[:, root_knots] - jnp.dot(
        solved[:, :root_knots],
        root_weight_means,
        precision=HIGHEST,
        preferred_element_type=jnp.float32,
    )
    mid_slab = knots_mid // regions
    middle_weight_means = lax.dynamic_slice_in_dim(group_mid, region * mid_slab, mid_slab, 0)[
        None, :
    ]
    fit_mid = jnp.dot(mid_basis, group_mid, precision=HIGHEST, preferred_element_type=jnp.float32)
    fit_root = jnp.dot(
        root_basis, root_weight_means, precision=HIGHEST, preferred_element_type=jnp.float32
    )
    return (root_weight_means, middle_weight_means, fit_mid + fit_root)


def solution(mesh):
    return jax.shard_map(
        on_device,
        mesh=mesh,
        in_specs=(
            P(("group", "region")),
            P(("group", "region")),
            P(("group", "region"), None),
            P(("group", "region"), None),
            P("group", None),
            P(),
            P("group", "region"),
        ),
        out_specs=(P(), P("group", "region"), P(("group", "region"))),
        check_vma=False,
    )
```

```python
import functools

import jax
import jax.numpy as jnp
from jax import lax
from jax.experimental import pallas as pl
from jax.experimental.pallas import tpu as pltpu
from jax.sharding import PartitionSpec as P

HIGHEST = lax.Precision.HIGHEST
HIGH = lax.Precision.HIGH
BLOCK = 128
PANEL = 8


def inner_gram(former, latter, precision):
    return lax.dot_general(
        former,
        latter,
        (((0,), (0,)), ((), ())),
        precision=precision,
        preferred_element_type=jnp.float32,
    )


def vector_product(vector, matrix):
    return jnp.dot(vector, matrix, precision=HIGHEST, preferred_element_type=jnp.float32)


def mxu(a, b):
    return jnp.dot(a, b, precision=HIGHEST, preferred_element_type=jnp.float32)


def negated_inverse(groups):
    count = len(groups)
    shape = (PANEL, count * PANEL)
    lane = lax.broadcasted_iota(jnp.int32, shape, 1)
    sub = lax.broadcasted_iota(jnp.int32, shape, 0)
    for p in range(count):
        rows = groups[p]
        first = p * PANEL
        inside = (lane >= first) & (lane < first + PANEL)
        cols = [jnp.broadcast_to(rows[:, first + k : first + k + 1], shape) for k in range(PANEL)]
        work = jnp.where(lane == first + sub, -1.0, jnp.where(inside, 0.0, rows))
        for k in range(PANEL):
            inv = 1.0 / jnp.broadcast_to(cols[k][k : k + 1, :], shape)
            own = sub == k
            factor = cols[k]
            for j in range(k + 1, PANEL):
                pivot_row = jnp.broadcast_to(cols[j][k : k + 1, :], shape) * inv
                cols[j] = jnp.where(own, pivot_row, cols[j] - factor * pivot_row)
            pivot_row = jnp.broadcast_to(work[k : k + 1, :], shape) * inv
            work = jnp.where(own, pivot_row, work - factor * pivot_row)
        spread = [jnp.broadcast_to(work[k : k + 1, :], shape) for k in range(PANEL)]
        order = [(p + 1 + i) % count for i in range(count - 1)]
        for i in order:
            value = jnp.where(inside, 0.0, groups[i])
            for k in range(PANEL):
                column = jnp.broadcast_to(groups[i][:, first + k : first + k + 1], shape)
                value = value - column * spread[k]
            groups[i] = value
        groups[p] = work
    return groups


def invert(a_ref, inv_ref, after=None):
    size = a_ref.shape[0]
    blocks = size // BLOCK
    rows = lax.broadcasted_iota(jnp.int32, (BLOCK, BLOCK), 0)
    cols = lax.broadcasted_iota(jnp.int32, (BLOCK, BLOCK), 1)
    unit = jnp.where(rows == cols, 1.0, 0.0)

    def step(kb, carry):
        start = pl.multiple_of(kb * BLOCK, BLOCK)
        own = pl.ds(start, BLOCK)
        diagonal = a_ref[own, own]
        groups = [diagonal[i * PANEL : (i + 1) * PANEL, :] for i in range(BLOCK // PANEL)]
        groups = negated_inverse(groups)
        for i, value in enumerate(groups):
            inv_ref[i * PANEL : (i + 1) * PANEL, :] = -value
        a_ref[own, own] = unit
        row = mxu(inv_ref[...], a_ref[own, :])
        for i in range(blocks):
            @pl.when(i != kb)
            def _():
                at = pl.ds(i * BLOCK, BLOCK)
                left = a_ref[at, own]
                a_ref[at, own] = jnp.zeros((BLOCK, BLOCK), jnp.float32)
                a_ref[at, :] = a_ref[at, :] - mxu(left, row)
        a_ref[own, :] = row
        if after is not None:
            pl.when(kb == 0)(after)
        return carry

    lax.fori_loop(0, blocks, step, 0)


def block_pairs(size):
    return [(i, j) for i in range(size // BLOCK) for j in range(i + 1)]


def span(i):
    return slice(i * BLOCK, (i + 1) * BLOCK)


def pack_symmetric(packed_ref, matrix_ref):
    for t, (i, j) in enumerate(block_pairs(matrix_ref.shape[0])):
        packed_ref[span(t), :] = matrix_ref[span(i), span(j)]


def unpack_symmetric(matrix_ref, packed_ref, prior_ref):
    rows = lax.broadcasted_iota(jnp.int32, (BLOCK, BLOCK), 0)
    cols = lax.broadcasted_iota(jnp.int32, (BLOCK, BLOCK), 1)
    for t, (i, j) in enumerate(block_pairs(matrix_ref.shape[0])):
        value = packed_ref[span(t), :]
        if i == j:
            value = value + jnp.where(rows == cols, prior_ref[:, span(i)], 0.0)
        else:
            matrix_ref[span(j), span(i)] = value.T
        matrix_ref[span(i), span(j)] = value


def pack_row(packed_ref, base, row_ref):
    tail = packed_ref.shape[0] - base
    packed_ref[base:, :] = jnp.zeros((tail, BLOCK), jnp.float32)
    for i in range(row_ref.shape[1] // BLOCK):
        packed_ref[base + i : base + i + 1, :] = row_ref[0:1, span(i)]


def unpack_row(packed_ref, base, size):
    parts = [packed_ref[base + i : base + i + 1, :] for i in range(size // BLOCK)]
    return jnp.broadcast_to(jnp.concatenate(parts, axis=1), (PANEL, size))


class Exchange:
    def __init__(self, regions, buffer, total, pair_land, half_sum, line_land, pair, line, slots):
        self.me = lax.axis_index("region")
        self.parity = self.me % 2
        self.place = self.me // 2
        self.line_count = regions // 2
        self.buffer, self.total = buffer, total
        self.pair_land, self.half_sum, self.line_land = pair_land, half_sum, line_land
        self.pair, self.line, self.slots = pair, line, slots
        rows = buffer.shape[0]
        self.half = rows // 2
        self.slab = self.half // self.line_count

    def half_at(self, parity):
        return pl.ds(pl.multiple_of(parity * self.half, PANEL), self.half)

    def slab_at(self):
        start = self.parity * self.half + self.place * self.slab
        return pl.ds(pl.multiple_of(start, PANEL), self.slab)

    def pair_copy(self, slot, source, target):
        return pltpu.make_async_remote_copy(
            src_ref=source,
            dst_ref=target,
            send_sem=self.pair[0].at[slot],
            recv_sem=self.pair[1].at[slot],
            device_id={"region": self.me + 1 - 2 * self.parity},
            device_id_type=pl.DeviceIdType.MESH,
        )

    def line_copy(self, slot, d, source, target):
        place = (self.place + d) % self.line_count
        return pltpu.make_async_remote_copy(
            src_ref=source(place),
            dst_ref=target,
            send_sem=self.line[0].at[slot, d - 1],
            recv_sem=self.line[1].at[slot, d - 1],
            device_id={"region": place * 2 + self.parity},
            device_id_type=pl.DeviceIdType.MESH,
        )

    def start_pair(self):
        self.first = self.pair_copy(
            self.slots[0], self.buffer.at[self.half_at(1 - self.parity)], self.pair_land
        )
        self.first.start()

    def start_line(self):
        self.first.wait()
        self.half_sum[...] = self.buffer[self.half_at(self.parity), :] + self.pair_land[...]

        def part(place):
            return self.half_sum.at[
                pl.ds(pl.multiple_of(place * self.slab, PANEL), self.slab)
            ]

        self.second = [
            self.line_copy(self.slots[1], d, part, self.line_land.at[d - 1])
            for d in range(1, self.line_count)
        ]
        for copy in self.second:
            copy.start()

    def slab_sum(self):
        for copy in self.second:
            copy.wait()
        own = pl.ds(pl.multiple_of(self.place * self.slab, PANEL), self.slab)
        value = self.half_sum[own, :]
        for d in range(1, self.line_count):
            value = value + self.line_land[d - 1]
        return value

    def start_line_gather(self, value):
        own = self.slab_at()
        self.total[own, :] = value
        self.third = [
            self.line_copy(self.slots[2], d, lambda place: self.total.at[own], self.total.at[own])
            for d in range(1, self.line_count)
        ]
        for copy in self.third:
            copy.start()

    def start_pair_gather(self):
        for copy in self.third:
            copy.wait()
        mine = self.total.at[self.half_at(self.parity)]
        self.fourth = self.pair_copy(self.slots[3], mine, mine)
        self.fourth.start()

    def finish(self):
        self.fourth.wait()


def mid_kernel(
    regions, members,
    gram_ref, cross_ref, rhs_ref, root_ref, root_rhs_ref, prior_ref,
    solved_ref, solved_rhs_ref, packed_ref,
    gram_buf, gram_sum, gram_pair, gram_half, gram_line,
    cross_buf, cross_sum, cross_pair, cross_half, cross_line,
    root_buf, root_sum, root_pair, root_half, root_line,
    inverse_ref, inv_ref, full_ref, work_ref, land_ref,
    pair_send, pair_recv, line_send, line_recv, group_send, group_recv,
):
    knots = gram_ref.shape[0]
    roots = root_ref.shape[0]
    me = lax.axis_index("region")
    group = lax.axis_index("group")
    line_count = regions // 2
    steps = members.bit_length() - 1
    partners = []
    for s in range(steps):
        bit = 1 << s
        partners.append(group + bit * (1 - 2 * ((group // bit) % 2)))
    barrier = pltpu.get_barrier_semaphore()
    for partner in partners:
        pl.semaphore_signal(
            barrier, inc=1, device_id={"group": partner}, device_id_type=pl.DeviceIdType.MESH
        )
    peers = [me + 1 - 2 * (me % 2)]
    for d in range(1, line_count):
        peers.append((me // 2 + d) % line_count * 2 + me % 2)
    for peer in peers:
        pl.semaphore_signal(
            barrier, inc=1, device_id={"region": peer}, device_id_type=pl.DeviceIdType.MESH
        )
    pair = (pair_send, pair_recv)
    line = (line_send, line_recv)
    gram = Exchange(regions, gram_buf, gram_sum, gram_pair, gram_half, gram_line, pair, line, (0, 0, 1, 1))
    cross = Exchange(regions, cross_buf, cross_sum, cross_pair, cross_half, cross_line, pair, line, (2, 2, 3, 3))
    root = Exchange(regions, root_buf, root_sum, root_pair, root_half, root_line, pair, line, (4, 4, 5, 5))

    pack_symmetric(gram_buf, gram_ref)
    used = len(block_pairs(knots)) * BLOCK
    if used < gram_buf.shape[0]:
        gram_buf[used:, :] = jnp.zeros((gram_buf.shape[0] - used, BLOCK), jnp.float32)
    pl.semaphore_wait(barrier, steps + line_count)
    gram.start_pair()
    cross_base = roots // BLOCK * knots
    for j in range(roots // BLOCK):
        cross_buf[j * knots : (j + 1) * knots, :] = cross_ref[:, span(j)]
    pack_row(cross_buf, cross_base, rhs_ref)
    cross.start_pair()
    gram.start_line()
    root_base = len(block_pairs(roots)) * BLOCK
    pack_symmetric(root_buf, root_ref)
    pack_row(root_buf, root_base, root_rhs_ref)
    gram.start_line_gather(gram.slab_sum())
    cross.start_line()
    gram.start_pair_gather()
    root.start_pair()
    cross.start_line_gather(cross.slab_sum())
    gram.finish()
    root.start_line()
    unpack_symmetric(inverse_ref, gram_sum, prior_ref)
    invert(inverse_ref, inv_ref)
    cross.start_pair_gather()
    cross.finish()
    for j in range(roots // BLOCK):
        full_ref[:, span(j)] = cross_sum[j * knots : (j + 1) * knots, :]
    solved_ref[...] = mxu(inverse_ref[...], full_ref[...])
    solved_rhs_ref[...] = mxu(unpack_row(cross_sum, cross_base, knots), inverse_ref[...])
    own_root = root.slab_sum()
    for t, (i, j) in enumerate(block_pairs(roots)):
        if j == 0:
            wide = (i + 1) * BLOCK
            rows = lax.dot_general(
                full_ref[:, span(i)],
                solved_ref[:, :wide],
                (((0,), (0,)), ((), ())),
                precision=HIGHEST,
                preferred_element_type=jnp.float32,
            )
        root_buf[span(t), :] = rows[:, span(j)]
    schur_rhs = mxu(solved_rhs_ref[...], full_ref[...])
    for i in range(roots // BLOCK):
        root_buf[root_base + i : root_base + i + 1, :] = schur_rhs[0:1, span(i)]
    for i in range(root_buf.shape[0] - root_base - roots // BLOCK):
        at = root_base + roots // BLOCK + i
        root_buf[at : at + 1, :] = jnp.zeros((1, BLOCK), jnp.float32)
    value = own_root - root_buf[root.slab_at(), :]
    for s, partner in enumerate(partners):
        work_ref[s] = value
        copy = pltpu.make_async_remote_copy(
            src_ref=work_ref.at[s],
            dst_ref=land_ref.at[s],
            send_sem=group_send.at[s],
            recv_sem=group_recv.at[s],
            device_id={"group": partner},
            device_id_type=pl.DeviceIdType.MESH,
        )
        copy.start()
        copy.wait()
        value = work_ref[s] + land_ref[s]
    root.start_line_gather(value)
    root.start_pair_gather()
    root.finish()
    packed_ref[...] = root_sum[...]


def root_kernel(packed_ref, prior_ref, solved_ref, solved_rhs_ref, root_out, mid_out, inverse_ref, inv_ref):
    roots = inverse_ref.shape[0]
    unpack_symmetric(inverse_ref, packed_ref, prior_ref)
    base = len(block_pairs(roots)) * BLOCK
    invert(inverse_ref, inv_ref)
    weights = mxu(unpack_row(packed_ref, base, roots), inverse_ref[...])
    root_out[...] = weights
    mid_out[...] = solved_rhs_ref[...] - lax.dot_general(
        weights,
        solved_ref[...],
        (((1,), (1,)), ((), ())),
        precision=HIGHEST,
        preferred_element_type=jnp.float32,
    )


def round_up(value, unit):
    return (value + unit - 1) // unit * unit


def mid_solve(gram, cross, rhs, root, root_rhs, prior):
    knots, roots = cross.shape
    regions = lax.axis_size("region")
    members = lax.axis_size("group")
    line_count = regions // 2
    steps = members.bit_length() - 1
    unit = PANEL * regions
    gram_rows = round_up(len(block_pairs(knots)) * BLOCK, unit)
    cross_rows = round_up(roots // BLOCK * knots + knots // BLOCK, unit)
    root_rows = round_up(len(block_pairs(roots)) * BLOCK + roots // BLOCK, unit)

    def vmem(*shape):
        return pltpu.VMEM(shape, jnp.float32)

    scratch = []
    for rows in (gram_rows, cross_rows, root_rows):
        scratch += [
            vmem(rows, BLOCK),
            vmem(rows, BLOCK),
            vmem(rows // 2, BLOCK),
            vmem(rows // 2, BLOCK),
            vmem(line_count - 1, rows // regions, BLOCK),
        ]
    scratch += [
        vmem(knots, knots),
        vmem(BLOCK, BLOCK),
        vmem(knots, roots),
        vmem(steps, root_rows // regions, BLOCK),
        vmem(steps, root_rows // regions, BLOCK),
        pltpu.SemaphoreType.DMA((6,)),
        pltpu.SemaphoreType.DMA((6,)),
        pltpu.SemaphoreType.DMA((6, line_count - 1)),
        pltpu.SemaphoreType.DMA((6, line_count - 1)),
        pltpu.SemaphoreType.DMA((steps,)),
        pltpu.SemaphoreType.DMA((steps,)),
    ]
    return pl.pallas_call(
        functools.partial(mid_kernel, regions, members),
        out_shape=(
            jax.ShapeDtypeStruct((knots, roots), jnp.float32),
            jax.ShapeDtypeStruct((PANEL, knots), jnp.float32),
            jax.ShapeDtypeStruct((root_rows, BLOCK), jnp.float32),
        ),
        scratch_shapes=scratch,
        compiler_params=pltpu.CompilerParams(collective_id=0, has_side_effects=True),
        name="mid_solve",
    )(gram, cross, rhs[None, :], root, root_rhs[None, :], prior[None, :])


def root_solve(packed, prior, solved, solved_rhs):
    knots, roots = solved.shape
    return pl.pallas_call(
        root_kernel,
        out_shape=(
            jax.ShapeDtypeStruct((PANEL, roots), jnp.float32),
            jax.ShapeDtypeStruct((PANEL, knots), jnp.float32),
        ),
        scratch_shapes=[
            pltpu.VMEM((roots, roots), jnp.float32),
            pltpu.VMEM((BLOCK, BLOCK), jnp.float32),
        ],
        name="root_solve",
    )(packed, prior[None, :], solved, solved_rhs)


def on_device(observed, noise_precision, mid_basis, root_basis, mid_prior, root_prior, leaf_count):
    leaf_slots = observed.shape[0]
    knots_mid = mid_basis.shape[1]
    live = (jnp.arange(leaf_slots, dtype=jnp.int32) < leaf_count[0, 0]).astype(jnp.float32)
    weight = noise_precision * live
    weighted_obs = observed * weight
    weighted_mid = mid_basis * weight[:, None]
    mid_gram = inner_gram(weighted_mid, mid_basis, HIGH)
    cross_gram = inner_gram(weighted_mid, root_basis, HIGH)
    mid_rhs = vector_product(weighted_obs, mid_basis)
    root_gram = inner_gram(root_basis * weight[:, None], root_basis, HIGH)
    root_rhs = vector_product(weighted_obs, root_basis)
    region = lax.axis_index("region")
    regions = lax.axis_size("region")
    solved, solved_rhs, packed = mid_solve(
        mid_gram, cross_gram, mid_rhs, root_gram, root_rhs, mid_prior[0]
    )
    root_means, group_means = root_solve(packed, root_prior, solved, solved_rhs)
    root_weight_means = root_means[0]
    group_mid = group_means[0]
    mid_slab = knots_mid // regions
    middle_weight_means = lax.dynamic_slice_in_dim(group_mid, region * mid_slab, mid_slab, 0)[
        None, :
    ]
    fit_mid = jnp.dot(mid_basis, group_mid, precision=HIGHEST, preferred_element_type=jnp.float32)
    fit_root = jnp.dot(
        root_basis, root_weight_means, precision=HIGHEST, preferred_element_type=jnp.float32
    )
    return (root_weight_means, middle_weight_means, fit_mid + fit_root)


def solution(mesh):
    return jax.shard_map(
        on_device,
        mesh=mesh,
        in_specs=(
            P(("group", "region")),
            P(("group", "region")),
            P(("group", "region"), None),
            P(("group", "region"), None),
            P("group", None),
            P(),
            P("group", "region"),
        ),
        out_specs=(P(), P("group", "region"), P(("group", "region"))),
        check_vma=False,
    )
```

```python
import functools

import jax
import jax.numpy as jnp
from jax import lax
from jax.experimental import pallas as pl
from jax.experimental.pallas import tpu as pltpu
from jax.sharding import PartitionSpec as P

HIGHEST = lax.Precision.HIGHEST
HIGH = lax.Precision.HIGH
BLOCK = 128
PANEL = 8


def inner_gram(former, latter, precision):
    return lax.dot_general(
        former,
        latter,
        (((0,), (0,)), ((), ())),
        precision=precision,
        preferred_element_type=jnp.float32,
    )


def mxu(a, b):
    return jnp.dot(a, b, precision=HIGHEST, preferred_element_type=jnp.float32)


def negated_inverse(groups):
    count = len(groups)
    shape = (PANEL, count * PANEL)
    lane = lax.broadcasted_iota(jnp.int32, shape, 1)
    sub = lax.broadcasted_iota(jnp.int32, shape, 0)
    for p in range(count):
        rows = groups[p]
        first = p * PANEL
        inside = (lane >= first) & (lane < first + PANEL)
        cols = [jnp.broadcast_to(rows[:, first + k : first + k + 1], shape) for k in range(PANEL)]
        work = jnp.where(lane == first + sub, -1.0, jnp.where(inside, 0.0, rows))
        for k in range(0, PANEL, 2):
            left, right = cols[k], cols[k + 1]
            top = jnp.broadcast_to(left[k : k + 1, :], shape)
            side = jnp.broadcast_to(right[k : k + 1, :], shape)
            low = jnp.broadcast_to(right[k + 1 : k + 2, :], shape)
            inv = 1.0 / (top * low - side * side)
            inv_top = 1.0 / top

            def cleared(target):
                upper = jnp.broadcast_to(target[k : k + 1, :], shape)
                lower = jnp.broadcast_to(target[k + 1 : k + 2, :], shape)
                new_lower = (top * lower - side * upper) * inv
                new_upper = (upper - side * new_lower) * inv_top
                rest = target - left * new_upper - right * new_lower
                return jnp.where(sub == k, new_upper, jnp.where(sub == k + 1, new_lower, rest))

            for j in range(k + 2, PANEL):
                cols[j] = cleared(cols[j])
            work = cleared(work)
        spread = [jnp.broadcast_to(work[k : k + 1, :], shape) for k in range(PANEL)]
        order = [(p + 1 + i) % count for i in range(count - 1)]
        for i in order:
            value = jnp.where(inside, 0.0, groups[i])
            for k in range(PANEL):
                column = jnp.broadcast_to(groups[i][:, first + k : first + k + 1], shape)
                value = value - column * spread[k]
            groups[i] = value
        groups[p] = work
    return groups


def invert(a_ref, inv_ref, after=None):
    size = a_ref.shape[0]
    blocks = size // BLOCK
    rows = lax.broadcasted_iota(jnp.int32, (BLOCK, BLOCK), 0)
    cols = lax.broadcasted_iota(jnp.int32, (BLOCK, BLOCK), 1)
    unit = jnp.where(rows == cols, 1.0, 0.0)

    def step(kb, carry):
        start = pl.multiple_of(kb * BLOCK, BLOCK)
        own = pl.ds(start, BLOCK)
        diagonal = a_ref[own, own]
        groups = [diagonal[i * PANEL : (i + 1) * PANEL, :] for i in range(BLOCK // PANEL)]
        groups = negated_inverse(groups)
        for i, value in enumerate(groups):
            inv_ref[i * PANEL : (i + 1) * PANEL, :] = -value
        a_ref[own, own] = unit
        row = mxu(inv_ref[...], a_ref[own, :])
        for i in range(blocks):
            @pl.when(i != kb)
            def _():
                at = pl.ds(i * BLOCK, BLOCK)
                left = a_ref[at, own]
                a_ref[at, own] = jnp.zeros((BLOCK, BLOCK), jnp.float32)
                a_ref[at, :] = a_ref[at, :] - mxu(left, row)
        a_ref[own, :] = row
        if after is not None:
            pl.when(kb == blocks // 2 - 1)(after)
        return carry

    lax.fori_loop(0, blocks, step, 0)


def block_pairs(size):
    return [(i, j) for i in range(size // BLOCK) for j in range(i + 1)]


def span(i):
    return slice(i * BLOCK, (i + 1) * BLOCK)


def pack_symmetric(packed_ref, matrix_ref):
    for t, (i, j) in enumerate(block_pairs(matrix_ref.shape[0])):
        packed_ref[span(t), :] = matrix_ref[span(i), span(j)]


def unpack_symmetric(matrix_ref, packed_ref, prior_ref):
    rows = lax.broadcasted_iota(jnp.int32, (BLOCK, BLOCK), 0)
    cols = lax.broadcasted_iota(jnp.int32, (BLOCK, BLOCK), 1)
    for t, (i, j) in enumerate(block_pairs(matrix_ref.shape[0])):
        value = packed_ref[span(t), :]
        if i == j:
            value = value + jnp.where(rows == cols, prior_ref[:, span(i)], 0.0)
        else:
            matrix_ref[span(j), span(i)] = value.T
        matrix_ref[span(i), span(j)] = value


def pack_row(packed_ref, base, row_ref):
    tail = packed_ref.shape[0] - base
    packed_ref[base:, :] = jnp.zeros((tail, BLOCK), jnp.float32)
    for i in range(row_ref.shape[1] // BLOCK):
        packed_ref[base + i : base + i + 1, :] = row_ref[0:1, span(i)]


def unpack_row(packed_ref, base, size):
    parts = [packed_ref[base + i : base + i + 1, :] for i in range(size // BLOCK)]
    return jnp.broadcast_to(jnp.concatenate(parts, axis=1), (PANEL, size))


class Exchange:
    def __init__(self, regions, buffer, total, pair_land, half_sum, line_land, pair, line, slots):
        self.me = lax.axis_index("region")
        self.parity = self.me % 2
        self.place = self.me // 2
        self.line_count = regions // 2
        self.buffer, self.total = buffer, total
        self.pair_land, self.half_sum, self.line_land = pair_land, half_sum, line_land
        self.pair, self.line, self.slots = pair, line, slots
        rows = buffer.shape[0]
        self.half = rows // 2
        self.slab = self.half // self.line_count

    def half_at(self, parity):
        return pl.ds(pl.multiple_of(parity * self.half, PANEL), self.half)

    def slab_at(self):
        start = self.parity * self.half + self.place * self.slab
        return pl.ds(pl.multiple_of(start, PANEL), self.slab)

    def pair_copy(self, slot, source, target):
        return pltpu.make_async_remote_copy(
            src_ref=source,
            dst_ref=target,
            send_sem=self.pair[0].at[slot],
            recv_sem=self.pair[1].at[slot],
            device_id={"region": self.me + 1 - 2 * self.parity},
            device_id_type=pl.DeviceIdType.MESH,
        )

    def line_copy(self, slot, d, source, target):
        place = (self.place + d) % self.line_count
        return pltpu.make_async_remote_copy(
            src_ref=source(place),
            dst_ref=target,
            send_sem=self.line[0].at[slot, d - 1],
            recv_sem=self.line[1].at[slot, d - 1],
            device_id={"region": place * 2 + self.parity},
            device_id_type=pl.DeviceIdType.MESH,
        )

    def start_pair(self):
        self.first = self.pair_copy(
            self.slots[0], self.buffer.at[self.half_at(1 - self.parity)], self.pair_land
        )
        self.first.start()

    def start_line(self):
        self.first.wait()
        self.half_sum[...] = self.buffer[self.half_at(self.parity), :] + self.pair_land[...]

        def part(place):
            return self.half_sum.at[
                pl.ds(pl.multiple_of(place * self.slab, PANEL), self.slab)
            ]

        self.second = [
            self.line_copy(self.slots[1], d, part, self.line_land.at[d - 1])
            for d in range(1, self.line_count)
        ]
        for copy in self.second:
            copy.start()

    def slab_sum(self):
        for copy in self.second:
            copy.wait()
        own = pl.ds(pl.multiple_of(self.place * self.slab, PANEL), self.slab)
        value = self.half_sum[own, :]
        for d in range(1, self.line_count):
            value = value + self.line_land[d - 1]
        return value

    def start_line_gather(self, value):
        own = self.slab_at()
        self.total[own, :] = value
        self.third = [
            self.line_copy(self.slots[2], d, lambda place: self.total.at[own], self.total.at[own])
            for d in range(1, self.line_count)
        ]
        for copy in self.third:
            copy.start()

    def start_pair_gather(self):
        for copy in self.third:
            copy.wait()
        self.last().start()

    def last(self):
        mine = self.total.at[self.half_at(self.parity)]
        return self.pair_copy(self.slots[3], mine, mine)

    def finish(self):
        self.last().wait()


def mid_kernel(
    regions, members,
    gram_ref, cross_ref, rhs_ref, root_ref, root_rhs_ref, prior_ref,
    solved_ref, solved_rhs_ref, packed_ref,
    gram_buf, gram_sum, gram_pair, gram_half, gram_line,
    cross_buf, cross_sum, cross_pair, cross_half, cross_line,
    root_buf, root_sum, root_pair, root_half, root_line,
    inverse_ref, inv_ref, full_ref, work_ref, land_ref,
    pair_send, pair_recv, line_send, line_recv, group_send, group_recv,
):
    knots = gram_ref.shape[0]
    roots = root_ref.shape[0]
    me = lax.axis_index("region")
    group = lax.axis_index("group")
    line_count = regions // 2
    steps = members.bit_length() - 1
    partners = []
    for s in range(steps):
        bit = 1 << s
        partners.append(group + bit * (1 - 2 * ((group // bit) % 2)))
    barrier = pltpu.get_barrier_semaphore()
    for partner in partners:
        pl.semaphore_signal(
            barrier, inc=1, device_id={"group": partner}, device_id_type=pl.DeviceIdType.MESH
        )
    peers = [me + 1 - 2 * (me % 2)]
    for d in range(1, line_count):
        peers.append((me // 2 + d) % line_count * 2 + me % 2)
    for peer in peers:
        pl.semaphore_signal(
            barrier, inc=1, device_id={"region": peer}, device_id_type=pl.DeviceIdType.MESH
        )
    pair = (pair_send, pair_recv)
    line = (line_send, line_recv)
    gram = Exchange(regions, gram_buf, gram_sum, gram_pair, gram_half, gram_line, pair, line, (0, 0, 1, 1))
    cross = Exchange(regions, cross_buf, cross_sum, cross_pair, cross_half, cross_line, pair, line, (2, 2, 3, 3))
    root = Exchange(regions, root_buf, root_sum, root_pair, root_half, root_line, pair, line, (4, 4, 5, 5))

    pack_symmetric(gram_buf, gram_ref)
    used = len(block_pairs(knots)) * BLOCK
    if used < gram_buf.shape[0]:
        gram_buf[used:, :] = jnp.zeros((gram_buf.shape[0] - used, BLOCK), jnp.float32)
    pl.semaphore_wait(barrier, steps + line_count)
    gram.start_pair()
    cross_base = roots // BLOCK * knots
    for j in range(roots // BLOCK):
        cross_buf[j * knots : (j + 1) * knots, :] = cross_ref[:, span(j)]
    pack_row(cross_buf, cross_base, rhs_ref)
    cross.start_pair()
    gram.start_line()
    root_base = len(block_pairs(roots)) * BLOCK
    pack_symmetric(root_buf, root_ref)
    pack_row(root_buf, root_base, root_rhs_ref)
    gram.start_line_gather(gram.slab_sum())
    cross.start_line()
    gram.start_pair_gather()
    root.start_pair()
    cross.start_line_gather(cross.slab_sum())
    gram.finish()
    root.start_line()
    unpack_symmetric(inverse_ref, gram_sum, prior_ref)
    invert(inverse_ref, inv_ref, cross.start_pair_gather)
    cross.finish()
    for j in range(roots // BLOCK):
        full_ref[:, span(j)] = cross_sum[j * knots : (j + 1) * knots, :]
    solved_ref[...] = mxu(inverse_ref[...], full_ref[...])
    solved_rhs_ref[...] = mxu(unpack_row(cross_sum, cross_base, knots), inverse_ref[...])
    own_root = root.slab_sum()
    for t, (i, j) in enumerate(block_pairs(roots)):
        if j == 0:
            wide = (i + 1) * BLOCK
            rows = lax.dot_general(
                full_ref[:, span(i)],
                solved_ref[:, :wide],
                (((0,), (0,)), ((), ())),
                precision=HIGHEST,
                preferred_element_type=jnp.float32,
            )
        root_buf[span(t), :] = rows[:, span(j)]
    schur_rhs = mxu(solved_rhs_ref[...], full_ref[...])
    for i in range(roots // BLOCK):
        root_buf[root_base + i : root_base + i + 1, :] = schur_rhs[0:1, span(i)]
    for i in range(root_buf.shape[0] - root_base - roots // BLOCK):
        at = root_base + roots // BLOCK + i
        root_buf[at : at + 1, :] = jnp.zeros((1, BLOCK), jnp.float32)
    value = own_root - root_buf[root.slab_at(), :]
    for s, partner in enumerate(partners):
        work_ref[s] = value
        copy = pltpu.make_async_remote_copy(
            src_ref=work_ref.at[s],
            dst_ref=land_ref.at[s],
            send_sem=group_send.at[s],
            recv_sem=group_recv.at[s],
            device_id={"group": partner},
            device_id_type=pl.DeviceIdType.MESH,
        )
        copy.start()
        copy.wait()
        value = work_ref[s] + land_ref[s]
    root.start_line_gather(value)
    root.start_pair_gather()
    root.finish()
    packed_ref[...] = root_sum[...]


def root_kernel(packed_ref, prior_ref, solved_ref, solved_rhs_ref, root_out, mid_out, inverse_ref, inv_ref):
    roots = inverse_ref.shape[0]
    unpack_symmetric(inverse_ref, packed_ref, prior_ref)
    base = len(block_pairs(roots)) * BLOCK
    invert(inverse_ref, inv_ref)
    weights = mxu(unpack_row(packed_ref, base, roots), inverse_ref[...])
    root_out[...] = weights
    mid_out[...] = solved_rhs_ref[...] - lax.dot_general(
        weights,
        solved_ref[...],
        (((1,), (1,)), ((), ())),
        precision=HIGHEST,
        preferred_element_type=jnp.float32,
    )


def round_up(value, unit):
    return (value + unit - 1) // unit * unit


def mid_solve(gram, cross, rhs, root, root_rhs, prior):
    knots, roots = cross.shape
    regions = lax.axis_size("region")
    members = lax.axis_size("group")
    line_count = regions // 2
    steps = members.bit_length() - 1
    unit = PANEL * regions
    gram_rows = round_up(len(block_pairs(knots)) * BLOCK, unit)
    cross_rows = round_up(roots // BLOCK * knots + knots // BLOCK, unit)
    root_rows = round_up(len(block_pairs(roots)) * BLOCK + roots // BLOCK, unit)

    def vmem(*shape):
        return pltpu.VMEM(shape, jnp.float32)

    scratch = []
    for rows in (gram_rows, cross_rows, root_rows):
        scratch += [
            vmem(rows, BLOCK),
            vmem(rows, BLOCK),
            vmem(rows // 2, BLOCK),
            vmem(rows // 2, BLOCK),
            vmem(line_count - 1, rows // regions, BLOCK),
        ]
    scratch += [
        vmem(knots, knots),
        vmem(BLOCK, BLOCK),
        vmem(knots, roots),
        vmem(steps, root_rows // regions, BLOCK),
        vmem(steps, root_rows // regions, BLOCK),
        pltpu.SemaphoreType.DMA((6,)),
        pltpu.SemaphoreType.DMA((6,)),
        pltpu.SemaphoreType.DMA((6, line_count - 1)),
        pltpu.SemaphoreType.DMA((6, line_count - 1)),
        pltpu.SemaphoreType.DMA((steps,)),
        pltpu.SemaphoreType.DMA((steps,)),
    ]
    return pl.pallas_call(
        functools.partial(mid_kernel, regions, members),
        out_shape=(
            jax.ShapeDtypeStruct((knots, roots), jnp.float32),
            jax.ShapeDtypeStruct((PANEL, knots), jnp.float32),
            jax.ShapeDtypeStruct((root_rows, BLOCK), jnp.float32),
        ),
        scratch_shapes=scratch,
        compiler_params=pltpu.CompilerParams(collective_id=0, has_side_effects=True),
        name="mid_solve",
    )(gram, cross, rhs[None, :], root, root_rhs[None, :], prior[None, :])


def root_solve(packed, prior, solved, solved_rhs):
    knots, roots = solved.shape
    return pl.pallas_call(
        root_kernel,
        out_shape=(
            jax.ShapeDtypeStruct((PANEL, roots), jnp.float32),
            jax.ShapeDtypeStruct((PANEL, knots), jnp.float32),
        ),
        scratch_shapes=[
            pltpu.VMEM((roots, roots), jnp.float32),
            pltpu.VMEM((BLOCK, BLOCK), jnp.float32),
        ],
        name="root_solve",
    )(packed, prior[None, :], solved, solved_rhs)


def on_device(observed, noise_precision, mid_basis, root_basis, mid_prior, root_prior, leaf_count):
    leaf_slots = observed.shape[0]
    knots_mid = mid_basis.shape[1]
    live = (jnp.arange(leaf_slots, dtype=jnp.int32) < leaf_count[0, 0]).astype(jnp.float32)
    weight = noise_precision * live
    weighted_obs = observed * weight
    weighted_mid = mid_basis * weight[:, None]
    mid_gram = inner_gram(weighted_mid, mid_basis, HIGH)
    cross_gram = inner_gram(weighted_mid, root_basis, HIGH)
    mid_rhs = jnp.sum(mid_basis * weighted_obs[:, None], axis=0)
    root_gram = inner_gram(root_basis * weight[:, None], root_basis, HIGH)
    root_rhs = jnp.sum(root_basis * weighted_obs[:, None], axis=0)
    region = lax.axis_index("region")
    regions = lax.axis_size("region")
    solved, solved_rhs, packed = mid_solve(
        mid_gram, cross_gram, mid_rhs, root_gram, root_rhs, mid_prior[0]
    )
    root_means, group_means = root_solve(packed, root_prior, solved, solved_rhs)
    root_weight_means = root_means[0]
    group_mid = group_means[0]
    mid_slab = knots_mid // regions
    middle_weight_means = lax.dynamic_slice_in_dim(group_mid, region * mid_slab, mid_slab, 0)[
        None, :
    ]
    leaf_fit = jnp.sum(
        mid_basis * group_mid[None, :] + root_basis * root_weight_means[None, :], axis=1
    )
    return (root_weight_means, middle_weight_means, leaf_fit)


def solution(mesh):
    return jax.shard_map(
        on_device,
        mesh=mesh,
        in_specs=(
            P(("group", "region")),
            P(("group", "region")),
            P(("group", "region"), None),
            P(("group", "region"), None),
            P("group", None),
            P(),
            P("group", "region"),
        ),
        out_specs=(P(), P("group", "region"), P(("group", "region"))),
        check_vma=False,
    )
```
